32 devices in a mesh: parts: 2 (over x), virt: 16 (over z, y, core).
Axes of the slice: x: 2, y: 2, z: 4, core: 2. Of those that a mesh axis runs over, the one named last changes fastest.
Arguments:
- trials: float32 [4096, 4, 256], P(('parts', 'virt')), parts along dimension 0, may hold values from -6 to 6
- vv_vectors: float32 [48, 2048, 2048], P('parts', 'virt'), parts along dimension 0, may hold values from -0.125 to 0.125
- oo_vectors: float32 [48, 256, 256], P('parts'), parts along dimension 0, may hold values from -0.078125 to 0.078125
- occ_energy: float32 [512], P('parts'), parts along dimension 0, may hold values from -2 to -0.5
- virt_energy: float32 [4096], P(('parts', 'virt')), parts along dimension 0, may hold values from 0.5 to 5, as said below
Outputs:
- filtered: float32 [4096, 4, 256], P(('parts', 'virt')), parts along dimension 0
- gram: float32 [8, 4], P('parts'), parts along dimension 0
The draws below stay inside these ranges and needn't reach their ends.
There are 2 independent parts, one for each index of `parts`. The reference program is written for one: setup_inputs(seed, part) draws one part's arguments, and reference() takes and returns one part's arrays. A program takes and returns all parts, laid end to end along the dimension named above; each array names one. Nothing has to cross between parts.
Inputs may be any that keep to these rules, and one draw needn't show every extreme that they name: `virt_energy`: rises with the orbital index, with a rough jitter.
All inputs are finite; a program needn't handle non-finite values.
Results may differ from the reference program's by a relative error of at most 0.0001.
Values sent between devices are 32-bit elements; how exact they have to be, the bound alone decides.
A program may use at most 128 MiB of HBM per device.

```python
import jax
import jax.numpy as jnp
from jax import lax

O = 256
V = 2048
K = 4
NVEC = 24


def draw_virt_energy(key, part):
    ladder = 0.5 + 3.5 * jnp.arange(V, dtype=jnp.float32) / V
    jitter = jax.random.uniform(key, (V,), jnp.float32, 0.0, 0.5)
    return ladder + jitter


def shard_levels(rng, dims, cuts, smallest, top_value):
    def one(position, shards_of):
        steps = jax.random.uniform(jax.random.fold_in(jax.random.fold_in(rng, 6), position), (shards_of,), jnp.float32, smallest / len(cuts), top_value / len(cuts))
        return jnp.repeat(jnp.exp(steps), dims[position] // shards_of).reshape((-1,) + (1,) * (len(dims) - position - 1))

    level = one(*cuts[0])
    for cut in cuts[1:]:
        level = level * one(*cut)
    return level


def centred(own_key, shape, scale, most, cuts=(), held_as=jnp.bfloat16):
    entries = scale * jax.random.normal(own_key, shape, jnp.float32)
    if cuts:
        entries = entries * shard_levels(own_key, shape, cuts, -0.22, 0.18)
    return jnp.clip(entries, -most, most).astype(held_as)


def setup_inputs(seed: int = 0, part: int = 0) -> dict:
    splits = jax.random.split(jax.random.key(seed), 6)
    part_splits = jax.random.split(jax.random.fold_in(splits[5], part), 6)
    return {
        "trials": centred(part_splits[0], (V, K, O), 1.0, 6.0, ((0, 16),), jnp.float32),
        "vv_vectors": centred(part_splits[1], (NVEC, V, V), V ** -0.5, 0.125, ((1, 16),), jnp.float32),
        "oo_vectors": centred(part_splits[2], (NVEC, O, O), (O * NVEC) ** -0.5, 0.078125, (), jnp.float32),
        "occ_energy": jnp.clip(jax.random.uniform(part_splits[3], (O,), jnp.float32, -2.0, -0.5), -2.0, -0.5),
        "virt_energy": draw_virt_energy(jax.random.fold_in(jax.random.fold_in(splits[5], part), 71), part),
    }


HIGH = lax.Precision.HIGHEST


def apply_operator(trial_block, vv_vectors, oo_vectors, energy_gap):
    flattened = trial_block.reshape(V, K * O)

    def per_vector(running, vectors):
        vv_one, oo_one = vectors
        half_image = jnp.dot(vv_one, flattened, precision=HIGH).reshape(V, K, O)
        return running + jnp.einsum("akj,ji->aki", half_image, oo_one, precision=HIGH), None

    direct, _ = lax.scan(per_vector, jnp.zeros((V, K, O), jnp.float32), (vv_vectors, oo_vectors))
    return energy_gap * trial_block - direct


def reference(trials, vv_vectors, oo_vectors, occ_energy, virt_energy):
    energy_gap = (virt_energy[:, None] - occ_energy[None, :])[:, None, :]
    first = (apply_operator(trials, vv_vectors, oo_vectors, energy_gap) - 4.5 * trials) / 3.0
    filtered = 2.0 * (apply_operator(first, vv_vectors, oo_vectors, energy_gap) - 4.5 * first) / 3.0 - trials
    gram = jnp.einsum("aki,ali->kl", filtered, filtered, precision=HIGH) / (O * V)
    return filtered, gram
```

```python
import functools

import jax
import jax.numpy as jnp
from jax import lax
from jax.experimental import pallas as pl
from jax.experimental.pallas import tpu as pltpu
from jax.sharding import PartitionSpec as P

HIGH = lax.Precision.HIGH


def sum_kernel(n, part_ref, out_ref, slots, send_sem, recv_sem, own_sem):
    me = lax.axis_index("virt")
    barrier = pltpu.get_barrier_semaphore()

    def greet(s, carry):
        pl.semaphore_signal(barrier, inc=1, device_id={"virt": lax.rem(me + s, n)})
        return carry

    lax.fori_loop(1, n, greet, 0)
    pl.semaphore_wait(barrier, n - 1)
    own = pltpu.make_async_copy(part_ref, slots.at[me], own_sem)
    own.start()

    def send(s, carry):
        pltpu.make_async_remote_copy(
            src_ref=part_ref,
            dst_ref=slots.at[me],
            send_sem=send_sem,
            recv_sem=recv_sem,
            device_id={"virt": lax.rem(me + s, n)},
        ).start()
        return carry

    lax.fori_loop(1, n, send, 0)
    own.wait()
    rest = slots.at[pl.ds(0, n - 1)]
    pltpu.make_async_copy(rest, rest, recv_sem).wait()
    out_ref[...] = jnp.sum(slots[...], axis=0)
    pltpu.make_async_copy(rest, rest, send_sem).wait()


def sum_over_virt(part):
    n = lax.axis_size("virt")
    return pl.pallas_call(
        functools.partial(sum_kernel, n),
        out_shape=jax.ShapeDtypeStruct(part.shape, part.dtype),
        in_specs=[pl.BlockSpec(memory_space=pltpu.VMEM)],
        out_specs=pl.BlockSpec(memory_space=pltpu.VMEM),
        scratch_shapes=[
            pltpu.VMEM((n,) + part.shape, part.dtype),
            pltpu.SemaphoreType.DMA,
            pltpu.SemaphoreType.DMA,
            pltpu.SemaphoreType.DMA,
        ],
        compiler_params=pltpu.CompilerParams(collective_id=0, has_side_effects=True),
        name="sum_over_virt",
    )(part)


def apply_operator(block, vv_vectors, oo_vectors, energy_gap):
    gathered = lax.all_gather(block, "virt", axis=0, tiled=True)
    half_image = jnp.einsum("pab,bj->paj", vv_vectors, gathered, precision=HIGH)
    direct = jnp.einsum("paj,pji->ai", half_image, oo_vectors, precision=HIGH)
    return energy_gap * block - direct


def per_device(trials, vv_vectors, oo_vectors, occ_energy, virt_energy):
    energy_gap = virt_energy[:, None] - occ_energy[None, :]
    count = trials.shape[1]
    blocks = [trials[:, k, :] for k in range(count)]
    first = [
        (apply_operator(b, vv_vectors, oo_vectors, energy_gap) - 4.5 * b) / 3.0
        for b in blocks
    ]
    pieces = [
        2.0 * (apply_operator(f, vv_vectors, oo_vectors, energy_gap) - 4.5 * f) / 3.0 - b
        for f, b in zip(first, blocks)
    ]
    filtered = jnp.stack(pieces, axis=1)
    rows = [
        jnp.stack([jnp.sum(pieces[k] * pieces[l]) for l in range(count)])
        for k in range(count)
    ]
    partial_gram = jnp.stack(rows)
    padded = jnp.zeros((8, 128), jnp.float32).at[:count, :count].set(partial_gram)
    gram = sum_over_virt(padded)[:count, :count] / (
        occ_energy.shape[0] * trials.shape[0] * lax.axis_size("virt")
    )
    return (filtered, gram)


def solution(mesh):
    in_specs = (
        P(("parts", "virt"), None, None),
        P("parts", "virt", None),
        P("parts", None, None),
        P("parts"),
        P(("parts", "virt")),
    )
    out_specs = (P(("parts", "virt"), None, None), P("parts", None))
    return jax.shard_map(
        per_device, mesh=mesh, in_specs=in_specs, out_specs=out_specs, check_vma=False
    )
```

```python
import functools

import jax
import jax.numpy as jnp
from jax import lax
from jax.experimental import pallas as pl
from jax.experimental.pallas import tpu as pltpu
from jax.sharding import PartitionSpec as P

AHEAD_Y = 4
AHEAD_C = 2
STAGES = 8
ROW_TILE = 768


def halves(x):
    high = x.astype(jnp.bfloat16)
    low = (x - high.astype(jnp.float32)).astype(jnp.bfloat16)
    return high, low


def kernel(sizes, trials, vv, oo, gap, out, gram, vh, vl, oh, ol, yh, yl, slots, acc,
           vstage, ostage, tile, tiles, v_sem, o_sem, own_sem, sz, sy, sc, rz, ry, rc, sg, rg, og):
    n, lines, across, count, rows, width, vectors, group = sizes
    groups = 2 * count
    steps = groups * lines
    me = lax.axis_index("virt")
    core = lax.rem(me, 2)
    chip = me // 2
    my_b = lax.rem(chip, across)
    my_a = chip // across
    partner = me + 1 - 2 * core

    def place(b, c):
        return pl.ds(pl.multiple_of((b * 2 + c) * rows, rows), rows)

    def device(a, b, c):
        return {"virt": (a * across + b) * 2 + c}

    barrier = pltpu.get_barrier_semaphore()

    def greet(s, carry):
        pl.semaphore_signal(barrier, inc=1, device_id={"virt": lax.rem(me + s, n)})
        return carry

    def v_copy(q):
        i, p = q // vectors, lax.rem(q, vectors)
        a = lax.rem(my_a + i, lines)
        slot = lax.rem(q, STAGES)
        return pltpu.make_async_copy(
            vv.at[p, :, pl.ds(pl.multiple_of(a * group, group), group)],
            vstage.at[slot], v_sem.at[slot])

    def o_copy(p):
        slot = lax.rem(p, 4)
        return pltpu.make_async_copy(oo.at[p], ostage.at[slot], o_sem.at[slot])

    for q in range(STAGES):
        v_copy(jnp.int32(q)).start()
    for p in range(4):
        o_copy(jnp.int32(p)).start()
    lax.fori_loop(1, n, greet, 0)
    pl.semaphore_wait(barrier, n - 1)

    def z_send(g, src):
        for j in range(1, lines):
            a = lax.rem(my_a + j, lines)
            pltpu.make_async_remote_copy(
                src_ref=src, dst_ref=slots.at[g, my_a, place(my_b, core)],
                send_sem=sz.at[g], recv_sem=rz.at[g, my_a],
                device_id=device(a, my_b, core)).start()

    def wait_bytes(amount, sem):
        ref = slots.at[0, 0, pl.ds(0, amount)]
        pltpu.make_async_copy(ref, ref, sem).wait()

    def y_forward(s):
        g, i = s // lines, lax.rem(s, lines)
        a = lax.rem(my_a + i, lines)

        @pl.when(i != 0)
        def _():
            wait_bytes(rows, rz.at[g, a])

        mine = slots.at[g, a, place(my_b, core)]
        for j in range(1, across):
            pltpu.make_async_remote_copy(
                src_ref=mine, dst_ref=mine, send_sem=sy.at[g], recv_sem=ry.at[g, a],
                device_id=device(my_a, lax.rem(my_b + j, across), core)).start()

    def c_forward(s):
        g, i = s // lines, lax.rem(s, lines)
        a = lax.rem(my_a + i, lines)
        wait_bytes((across - 1) * rows, ry.at[g, a])
        for b in range(across):
            block = slots.at[g, a, place(b, core)]
            pltpu.make_async_remote_copy(
                src_ref=block, dst_ref=block, send_sem=sc.at[g], recv_sem=rc.at[g, a],
                device_id={"virt": partner}).start()

    own = [
        pltpu.make_async_copy(
            trials.at[k], slots.at[k, my_a, place(my_b, core)], own_sem.at[k])
        for k in range(count)
    ]
    for k in range(count):
        own[k].start()
    for k in range(count):
        z_send(k, trials.at[k])
    for k in range(count):
        own[k].wait()
    y_forward(jnp.int32(0))

    def split_oo(p, carry):
        o_copy(p).wait()
        high, low = halves(ostage[lax.rem(p, 4)])
        oh[p] = high
        ol[p] = low

        @pl.when(p + 4 < vectors)
        def _():
            o_copy(p + 4).start()
        return carry

    lax.fori_loop(0, vectors, split_oo, 0)
    for s in range(1, AHEAD_Y):
        y_forward(jnp.int32(s))
        if s <= AHEAD_C:
            c_forward(jnp.int32(s - 1))

    def step(s, carry):
        g, i = s // lines, lax.rem(s, lines)
        a = lax.rem(my_a + i, lines)

        @pl.when(s + AHEAD_Y < steps)
        def _():
            y_forward(s + AHEAD_Y)

        @pl.when(s + AHEAD_C < steps)
        def _():
            c_forward(s + AHEAD_C)

        @pl.when(g == 0)
        def _():
            def split_vv(p, inner):
                q = i * vectors + p
                v_copy(q).wait()
                high, low = halves(vstage[lax.rem(q, STAGES)])
                where = pl.ds(pl.multiple_of(p * rows, rows), rows)
                vh[a, where] = high
                vl[a, where] = low

                @pl.when(q + STAGES < lines * vectors)
                def _():
                    v_copy(q + STAGES).start()
                return inner

            lax.fori_loop(0, vectors, split_vv, 0)

        wait_bytes(across * rows, rc.at[g, a])
        high, low = halves(slots[g, a])
        yh[...] = high
        yl[...] = low
        total_rows = vectors * rows
        tall = min(ROW_TILE, total_rows)

        def product(t, inner):
            where = pl.ds(pl.multiple_of(t * tall, tall), tall)
            top, rest = vh[a, where], vl[a, where]
            left = jnp.concatenate([top, top, rest], axis=1)
            right = jnp.concatenate([yh[...], yl[...], yh[...]], axis=0)
            term = jnp.dot(left, right, preferred_element_type=jnp.float32)
            acc[where] = jnp.where(i == 0, term, acc[where] + term)
            return inner

        lax.fori_loop(0, total_rows // tall, product, 0)

        @pl.when(i == lines - 1)
        def _():
            def second(p, running):
                zh, zl = halves(acc[pl.ds(pl.multiple_of(p * rows, rows), rows)])
                left = jnp.concatenate([zh, zh, zl], axis=1)
                right = jnp.concatenate([oh[p], ol[p], oh[p]], axis=0)
                return running + jnp.dot(left, right, preferred_element_type=jnp.float32)

            direct = lax.fori_loop(
                0, vectors, second, jnp.zeros((rows, width), jnp.float32), unroll=2)

            @pl.when(g < count)
            def _():
                y = trials[g]
                mine = slots.at[g + count, my_a, place(my_b, core)]
                mine[...] = ((gap[...] * y - direct) - 4.5 * y) / 3.0
                z_send(g + count, mine)

            @pl.when(g >= count)
            def _():
                y = slots[g, my_a, place(my_b, core)]
                out[g - count] = 2.0 * ((gap[...] * y - direct) - 4.5 * y) / 3.0 - trials[g - count]

        return carry

    lax.fori_loop(0, steps, step, 0)

    row = lax.broadcasted_iota(jnp.int32, tile.shape, 0)
    col = lax.broadcasted_iota(jnp.int32, tile.shape, 1)
    part = jnp.zeros(tile.shape, jnp.float32)
    for k in range(count):
        for l in range(k, count):
            value = jnp.sum(out[k] * out[l])
            hit = ((row == k) & (col == l)) | ((row == l) & (col == k))
            part = jnp.where(hit, value, part)
    tile[...] = part
    tiles[me] = part

    def send(s, carry):
        pltpu.make_async_remote_copy(
            src_ref=tile, dst_ref=tiles.at[me], send_sem=sg, recv_sem=rg,
            device_id={"virt": lax.rem(me + s, n)}).start()
        return carry

    lax.fori_loop(1, n, send, 0)
    for g in range(groups):
        wait_bytes((lines - 1) * rows, sz.at[g])
        for _ in range(across - 1):
            wait_bytes(lines * rows, sy.at[g])
        for _ in range(across):
            wait_bytes(lines * rows, sc.at[g])
    others = tiles.at[pl.ds(0, n - 1)]
    pltpu.make_async_copy(others, others, rg).wait()
    gram[...] = jnp.sum(tiles[...], axis=0) / (n * rows * width)
    pltpu.make_async_copy(others, others, sg).wait()


def per_device(trials, vv_vectors, oo_vectors, occ_energy, virt_energy):
    n = lax.axis_size("virt")
    rows, count, width = trials.shape
    vectors = vv_vectors.shape[0]
    chips = n // 2
    across = 1
    while across * across * 4 <= chips:
        across *= 2
    across = max(across, 2)
    lines = chips // across
    group = across * 2 * rows
    gap = virt_energy[:, None] - occ_energy[None, :]
    sizes = (n, lines, across, count, rows, width, vectors, group)
    groups = 2 * count
    f32, bf16 = jnp.float32, jnp.bfloat16
    dma = pltpu.SemaphoreType.DMA
    vmem = pl.BlockSpec(memory_space=pltpu.VMEM)
    hbm = pl.BlockSpec(memory_space=pl.ANY)
    out, gram = pl.pallas_call(
        functools.partial(kernel, sizes),
        out_shape=(
            jax.ShapeDtypeStruct((count, rows, width), f32),
            jax.ShapeDtypeStruct((8, 128), f32),
        ),
        in_specs=[vmem, hbm, hbm, vmem],
        out_specs=(vmem, vmem),
        scratch_shapes=[
            pltpu.VMEM((lines, vectors * rows, group), bf16),
            pltpu.VMEM((lines, vectors * rows, group), bf16),
            pltpu.VMEM((vectors, width, width), bf16),
            pltpu.VMEM((vectors, width, width), bf16),
            pltpu.VMEM((group, width), bf16),
            pltpu.VMEM((group, width), bf16),
            pltpu.VMEM((groups, lines, group, width), f32),
            pltpu.VMEM((vectors * rows, width), f32),
            pltpu.VMEM((STAGES, rows, group), f32),
            pltpu.VMEM((4, width, width), f32),
            pltpu.VMEM((8, 128), f32),
            pltpu.VMEM((n, 8, 128), f32),
            dma((STAGES,)), dma((4,)), dma((count,)),
            dma((groups,)), dma((groups,)), dma((groups,)),
            dma((groups, lines)), dma((groups, lines)), dma((groups, lines)),
            dma, dma, dma,
        ],
        compiler_params=pltpu.CompilerParams(
            collective_id=0, has_side_effects=True, vmem_limit_bytes=63 * 2**20),
        name="filter_step",
    )(jnp.transpose(trials, (1, 0, 2)), vv_vectors, oo_vectors, gap)
    return (jnp.transpose(out, (1, 0, 2)), gram[:count, :count])


def solution(mesh):
    in_specs = (
        P(("parts", "virt"), None, None),
        P("parts", "virt", None),
        P("parts", None, None),
        P("parts"),
        P(("parts", "virt")),
    )
    out_specs = (P(("parts", "virt"), None, None), P("parts", None))
    return jax.shard_map(
        per_device, mesh=mesh, in_specs=in_specs, out_specs=out_specs, check_vma=False
    )
```

```python
import functools

import jax
import jax.numpy as jnp
from jax import lax
from jax.experimental import pallas as pl
from jax.experimental.pallas import tpu as pltpu
from jax.sharding import PartitionSpec as P

AHEAD_Y = 4
AHEAD_C = 2
STAGES = 8
ROW_TILE = 768
TOGETHER = 8


def halves(x):
    high = x.astype(jnp.bfloat16)
    low = (x - high.astype(jnp.float32)).astype(jnp.bfloat16)
    return high, low


def kernel(sizes, trials, vv, oo, gap, out, gram, vh, vl, oh, ol, yh, yl, slots, acc,
           vstage, ostage, tile, tiles, v_sem, o_sem, own_sem, sz, sy, sc, rz, ry, rc, sg, rg, og):
    n, lines, across, count, rows, width, vectors, group = sizes
    groups = 2 * count
    steps = groups * lines
    me = lax.axis_index("virt")
    core = lax.rem(me, 2)
    chip = me // 2
    my_b = lax.rem(chip, across)
    my_a = chip // across
    partner = me + 1 - 2 * core

    def place(b, c):
        return pl.ds(pl.multiple_of((b * 2 + c) * rows, rows), rows)

    def device(a, b, c):
        return {"virt": (a * across + b) * 2 + c}

    barrier = pltpu.get_barrier_semaphore()

    def greet(s, carry):
        pl.semaphore_signal(barrier, inc=1, device_id={"virt": lax.rem(me + s, n)})
        return carry

    def v_copy(q):
        i, p = q // vectors, lax.rem(q, vectors)
        a = lax.rem(my_a + i, lines)
        slot = lax.rem(q, STAGES)
        return pltpu.make_async_copy(
            vv.at[p, :, pl.ds(pl.multiple_of(a * group, group), group)],
            vstage.at[slot], v_sem.at[slot])

    def o_copy(p):
        slot = lax.rem(p, 4)
        return pltpu.make_async_copy(oo.at[p], ostage.at[slot], o_sem.at[slot])

    for q in range(STAGES):
        v_copy(jnp.int32(q)).start()
    for p in range(4):
        o_copy(jnp.int32(p)).start()
    lax.fori_loop(1, n, greet, 0)
    pl.semaphore_wait(barrier, n - 1)

    def z_send(g, src):
        for j in range(1, lines):
            a = lax.rem(my_a + j, lines)
            pltpu.make_async_remote_copy(
                src_ref=src, dst_ref=slots.at[g, my_a, place(my_b, core)],
                send_sem=sz.at[g], recv_sem=rz.at[g, my_a],
                device_id=device(a, my_b, core)).start()

    def wait_bytes(amount, sem):
        ref = slots.at[0, 0, pl.ds(0, amount)]
        pltpu.make_async_copy(ref, ref, sem).wait()

    def y_forward(s):
        g, i = s // lines, lax.rem(s, lines)
        a = lax.rem(my_a + i, lines)

        @pl.when(i != 0)
        def _():
            wait_bytes(rows, rz.at[g, a])

        mine = slots.at[g, a, place(my_b, core)]
        for j in range(1, across):
            pltpu.make_async_remote_copy(
                src_ref=mine, dst_ref=mine, send_sem=sy.at[g], recv_sem=ry.at[g, a],
                device_id=device(my_a, lax.rem(my_b + j, across), core)).start()

    def c_forward(s):
        g, i = s // lines, lax.rem(s, lines)
        a = lax.rem(my_a + i, lines)
        wait_bytes((across - 1) * rows, ry.at[g, a])
        for b in range(across):
            block = slots.at[g, a, place(b, core)]
            pltpu.make_async_remote_copy(
                src_ref=block, dst_ref=block, send_sem=sc.at[g], recv_sem=rc.at[g, a],
                device_id={"virt": partner}).start()

    own = [
        pltpu.make_async_copy(
            trials.at[k], slots.at[k, my_a, place(my_b, core)], own_sem.at[k])
        for k in range(count)
    ]
    for k in range(count):
        own[k].start()
    for k in range(count):
        z_send(k, trials.at[k])
    for k in range(count):
        own[k].wait()
    y_forward(jnp.int32(0))

    def split_oo(p, carry):
        o_copy(p).wait()
        high, low = halves(ostage[lax.rem(p, 4)])
        oh[p] = high
        ol[p] = low

        @pl.when(p + 4 < vectors)
        def _():
            o_copy(p + 4).start()
        return carry

    lax.fori_loop(0, vectors, split_oo, 0)
    for s in range(1, AHEAD_Y):
        y_forward(jnp.int32(s))
        if s <= AHEAD_C:
            c_forward(jnp.int32(s - 1))

    def step(s, carry):
        g, i = s // lines, lax.rem(s, lines)
        a = lax.rem(my_a + i, lines)

        @pl.when(s + AHEAD_Y < steps)
        def _():
            y_forward(s + AHEAD_Y)

        @pl.when(s + AHEAD_C < steps)
        def _():
            c_forward(s + AHEAD_C)

        @pl.when(g == 0)
        def _():
            def split_vv(p, inner):
                q = i * vectors + p
                v_copy(q).wait()
                high, low = halves(vstage[lax.rem(q, STAGES)])
                where = pl.ds(pl.multiple_of(p * rows, rows), rows)
                vh[a, where] = high
                vl[a, where] = low

                @pl.when(q + STAGES < lines * vectors)
                def _():
                    v_copy(q + STAGES).start()
                return inner

            lax.fori_loop(0, vectors, split_vv, 0)

        wait_bytes(across * rows, rc.at[g, a])
        high, low = halves(slots[g, a])
        yh[...] = high
        yl[...] = low
        total_rows = vectors * rows
        tall = min(ROW_TILE, total_rows)

        for t in range(total_rows // tall):
            where = pl.ds(t * tall, tall)
            top, rest = vh[a, where], vl[a, where]
            left = jnp.concatenate([top, top, rest], axis=1)
            right = jnp.concatenate([yh[...], yl[...], yh[...]], axis=0)
            term = jnp.dot(left, right, preferred_element_type=jnp.float32)
            acc[where] = jnp.where(i == 0, term, acc[where] + term)

        @pl.when(i == lines - 1)
        def _():
            def second(q, running):
                left, right = [], []
                for u in range(TOGETHER):
                    p = q * TOGETHER + u
                    zh, zl = halves(acc[pl.ds(pl.multiple_of(p * rows, rows), rows)])
                    left += [zh, zh, zl]
                    right += [oh[p], ol[p], oh[p]]
                return running + jnp.dot(
                    jnp.concatenate(left, axis=1), jnp.concatenate(right, axis=0),
                    preferred_element_type=jnp.float32)

            direct = lax.fori_loop(
                0, vectors // TOGETHER, second, jnp.zeros((rows, width), jnp.float32))

            @pl.when(g < count)
            def _():
                y = trials[g]
                mine = slots.at[g + count, my_a, place(my_b, core)]
                mine[...] = ((gap[...] * y - direct) - 4.5 * y) / 3.0
                z_send(g + count, mine)

            @pl.when(g >= count)
            def _():
                y = slots[g, my_a, place(my_b, core)]
                out[g - count] = 2.0 * ((gap[...] * y - direct) - 4.5 * y) / 3.0 - trials[g - count]

        return carry

    lax.fori_loop(0, steps, step, 0)

    row = lax.broadcasted_iota(jnp.int32, tile.shape, 0)
    col = lax.broadcasted_iota(jnp.int32, tile.shape, 1)
    part = jnp.zeros(tile.shape, jnp.float32)
    for k in range(count):
        for l in range(k, count):
            value = jnp.sum(out[k] * out[l])
            hit = ((row == k) & (col == l)) | ((row == l) & (col == k))
            part = jnp.where(hit, value, part)
    tile[...] = part
    tiles[me] = part

    def send(s, carry):
        pltpu.make_async_remote_copy(
            src_ref=tile, dst_ref=tiles.at[me], send_sem=sg, recv_sem=rg,
            device_id={"virt": lax.rem(me + s, n)}).start()
        return carry

    lax.fori_loop(1, n, send, 0)
    for g in range(groups):
        wait_bytes((lines - 1) * rows, sz.at[g])
        for _ in range(across - 1):
            wait_bytes(lines * rows, sy.at[g])
        for _ in range(across):
            wait_bytes(lines * rows, sc.at[g])
    others = tiles.at[pl.ds(0, n - 1)]
    pltpu.make_async_copy(others, others, rg).wait()
    gram[...] = jnp.sum(tiles[...], axis=0) / (n * rows * width)
    pltpu.make_async_copy(others, others, sg).wait()


def per_device(trials, vv_vectors, oo_vectors, occ_energy, virt_energy):
    n = lax.axis_size("virt")
    rows, count, width = trials.shape
    vectors = vv_vectors.shape[0]
    chips = n // 2
    across = 1
    while across * across * 4 <= chips:
        across *= 2
    across = max(across, 2)
    lines = chips // across
    group = across * 2 * rows
    gap = virt_energy[:, None] - occ_energy[None, :]
    sizes = (n, lines, across, count, rows, width, vectors, group)
    groups = 2 * count
    f32, bf16 = jnp.float32, jnp.bfloat16
    dma = pltpu.SemaphoreType.DMA
    vmem = pl.BlockSpec(memory_space=pltpu.VMEM)
    hbm = pl.BlockSpec(memory_space=pl.ANY)
    out, gram = pl.pallas_call(
        functools.partial(kernel, sizes),
        out_shape=(
            jax.ShapeDtypeStruct((count, rows, width), f32),
            jax.ShapeDtypeStruct((8, 128), f32),
        ),
        in_specs=[vmem, hbm, hbm, vmem],
        out_specs=(vmem, vmem),
        scratch_shapes=[
            pltpu.VMEM((lines, vectors * rows, group), bf16),
            pltpu.VMEM((lines, vectors * rows, group), bf16),
            pltpu.VMEM((vectors, width, width), bf16),
            pltpu.VMEM((vectors, width, width), bf16),
            pltpu.VMEM((group, width), bf16),
            pltpu.VMEM((group, width), bf16),
            pltpu.VMEM((groups, lines, group, width), f32),
            pltpu.VMEM((vectors * rows, width), f32),
            pltpu.VMEM((STAGES, rows, group), f32),
            pltpu.VMEM((4, width, width), f32),
            pltpu.VMEM((8, 128), f32),
            pltpu.VMEM((n, 8, 128), f32),
            dma((STAGES,)), dma((4,)), dma((count,)),
            dma((groups,)), dma((groups,)), dma((groups,)),
            dma((groups, lines)), dma((groups, lines)), dma((groups, lines)),
            dma, dma, dma,
        ],
        compiler_params=pltpu.CompilerParams(
            collective_id=0, has_side_effects=True, vmem_limit_bytes=63 * 2**20),
        name="filter_step",
    )(jnp.transpose(trials, (1, 0, 2)), vv_vectors, oo_vectors, gap)
    return (jnp.transpose(out, (1, 0, 2)), gram[:count, :count])


def solution(mesh):
    in_specs = (
        P(("parts", "virt"), None, None),
        P("parts", "virt", None),
        P("parts", None, None),
        P("parts"),
        P(("parts", "virt")),
    )
    out_specs = (P(("parts", "virt"), None, None), P("parts", None))
    return jax.shard_map(
        per_device, mesh=mesh, in_specs=in_specs, out_specs=out_specs, check_vma=False
    )
```
